32 devices in a mesh: fsdp: 8 (over y, x, core), seq: 4 (over z).
Axes of the slice: x: 2, y: 2, z: 4, core: 2. Of those that a mesh axis runs over, the one named last changes fastest.
Arguments:
- x_in: bfloat16 [16, 512, 768], P('fsdp', 'seq'), may hold values from -6 to 6
- lengths: int32 [16], P('fsdp'), may hold values from 64 to 512, as said below
- w_query: bfloat16 [768, 768], P('fsdp'), may hold values from -0.21875 to 0.21875
- w_key: bfloat16 [768, 768], P('fsdp'), may hold values from -0.21875 to 0.21875
- w_value: bfloat16 [768, 768], P('fsdp'), may hold values from -0.21875 to 0.21875
- w_out: bfloat16 [768, 768], P('fsdp'), may hold values from -1.75 to 1.75
- w_up: bfloat16 [768, 3072], P('fsdp'), may hold values from -0.21875 to 0.21875
- w_down: bfloat16 [3072, 768], P('fsdp'), may hold values from -0.109375 to 0.109375
- b_query: float32 [768], P('fsdp'), may hold values from -3 to 3
- b_value: float32 [768], P('fsdp'), may hold values from -3 to 3
- b_out: float32 [768], P('fsdp'), may hold values from -3 to 3
- b_up: float32 [3072], P('fsdp'), may hold values from -3 to 3
- b_down: float32 [768], P('fsdp'), may hold values from -3 to 3
- ln1_gain: float32 [768], P('fsdp'), may hold values from 0.1 to 1.9
- ln1_shift: float32 [768], P('fsdp'), may hold values from -3 to 3
- ln2_gain: float32 [768], P('fsdp'), may hold values from 0.1 to 1.9
- ln2_shift: float32 [768], P('fsdp'), may hold values from -3 to 3
- d_out: bfloat16 [16, 512, 768], P('fsdp', 'seq'), may hold values from -6 to 6
Outputs:
- block_out: bfloat16 [16, 512, 768], P('fsdp', 'seq')
- d_input: float32 [16, 512, 768], P('fsdp', 'seq')
- d_w_query: float32 [768, 768], P('fsdp')
- d_w_key: float32 [768, 768], P('fsdp')
- d_w_value: float32 [768, 768], P('fsdp')
- d_w_out: float32 [768, 768], P('fsdp')
- d_w_up: float32 [768, 3072], P('fsdp')
- d_w_down: float32 [3072, 768], P('fsdp')
- d_b_query: float32 [768], P('fsdp')
- d_b_value: float32 [768], P('fsdp')
- d_b_out: float32 [768], P('fsdp')
- d_b_up: float32 [3072], P('fsdp')
- d_b_down: float32 [768], P('fsdp')
- d_ln1_gain: float32 [768], P('fsdp')
- d_ln1_shift: float32 [768], P('fsdp')
- d_ln2_gain: float32 [768], P('fsdp')
- d_ln2_shift: float32 [768], P('fsdp')
The draws below stay inside these ranges and needn't reach their ends.
Inputs may be any that keep to these rules, and one draw needn't show every extreme that they name: `lengths`: positions below a sequence's length are valid keys; some sequence is full and some has exactly 64 valid tokens.
All inputs are finite; a program needn't handle non-finite values.
Results may differ from the reference program's by a relative error of at most 0.038.
Values may be sent and summed in bfloat16 or wider, within the bound.
No kernel may reach another device: no remote copies, remote signals or barrier semaphores. Data moves between devices by JAX's collectives and lax.ppermute only.
A program may use at most 128 MiB of HBM per device.

```python
import jax
import jax.numpy as jnp
from jax import lax

D = 768
HEADS = 12
HD = 64
FF = 3072
L = 512
SEQS = 16


def draw_lengths(key, part):
    counts = jax.random.randint(jax.random.fold_in(key, 21), (SEQS,), L // 8, L + 1, dtype=jnp.int32)
    counts = counts.at[0].set(L)
    counts = counts.at[1].set(L // 8)
    return counts


def shard_levels(stream_key, extent, split, smallest, largest):
    level = 1.0
    for axis_at, shards_of in split:
        steps = jax.random.uniform(jax.random.fold_in(jax.random.fold_in(stream_key, 6), axis_at), (shards_of,), jnp.float32, smallest / len(split), largest / len(split))
        level = level * jnp.repeat(jnp.exp(steps), extent[axis_at] // shards_of).reshape((-1,) + (1,) * (len(extent) - 1 - axis_at))
    return level


def scatter_about(key, dims, deviation, reach, shards=(), kind=jnp.bfloat16):
    entries = jax.random.normal(key, dims, jnp.float32) * deviation
    if len(shards) > 0:
        entries = shard_levels(key, dims, shards, -0.22, 0.18) * entries
    return jnp.clip(entries, min=-reach, max=reach).astype(kind)


def setup_inputs(seed: int = 0) -> dict:
    streams_of = jax.random.split(jax.random.key(seed), 19)
    x_in = scatter_about(streams_of[0], (SEQS, L, D), 1.0, 6.0, ((0, 8), (1, 4)))
    lengths = draw_lengths(jax.random.fold_in(streams_of[18], 71), 0)
    w_query = scatter_about(streams_of[2], (D, D), D ** -0.5, 0.21875, ((0, 8),))
    w_key = scatter_about(streams_of[3], (D, D), D ** -0.5, 0.21875, ((0, 8),))
    w_value = scatter_about(streams_of[4], (D, D), D ** -0.5, 0.21875, ((0, 8),))
    w_out = scatter_about(streams_of[5], (D, D), (D // 64) ** -0.5, 1.75, ((0, 8),))
    w_up = scatter_about(streams_of[6], (D, FF), D ** -0.5, 0.21875, ((0, 8),))
    w_down = scatter_about(streams_of[7], (FF, D), FF ** -0.5, 0.109375, ((0, 8),))
    b_query = scatter_about(streams_of[8], (D,), 0.5, 3.0, ((0, 8),), jnp.float32)
    b_value = scatter_about(streams_of[9], (D,), 0.5, 3.0, ((0, 8),), jnp.float32)
    b_out = scatter_about(streams_of[10], (D,), 0.5, 3.0, ((0, 8),), jnp.float32)
    b_up = scatter_about(streams_of[11], (FF,), 0.5, 3.0, ((0, 8),), jnp.float32)
    b_down = scatter_about(streams_of[12], (D,), 0.5, 3.0, ((0, 8),), jnp.float32)
    ln1_gain = jnp.clip(1.0 + 0.18 * jax.random.normal(streams_of[13], (D,), jnp.float32), 0.1, 1.9)
    ln1_shift = scatter_about(streams_of[14], (D,), 0.5, 3.0, ((0, 8),), jnp.float32)
    ln2_gain = jnp.clip(1.0 + 0.18 * jax.random.normal(streams_of[15], (D,), jnp.float32), 0.1, 1.9)
    ln2_shift = scatter_about(streams_of[16], (D,), 0.5, 3.0, ((0, 8),), jnp.float32)
    d_out = scatter_about(streams_of[17], (SEQS, L, D), 1.0, 6.0, ((0, 8), (1, 4)))
    return {"x_in": x_in, "lengths": lengths, "w_query": w_query, "w_key": w_key, "w_value": w_value, "w_out": w_out, "w_up": w_up, "w_down": w_down, "b_query": b_query, "b_value": b_value, "b_out": b_out, "b_up": b_up, "b_down": b_down, "ln1_gain": ln1_gain, "ln1_shift": ln1_shift, "ln2_gain": ln2_gain, "ln2_shift": ln2_shift, "d_out": d_out}


EPS = 1e-05

def layer_norm(values_in, gain, shift):
    mean_val = lax.optimization_barrier(jnp.mean(values_in, axis=-1, keepdims=True))
    centred = values_in - mean_val
    variance = lax.optimization_barrier(jnp.mean(centred * centred, axis=-1, keepdims=True))
    inverse = lax.rsqrt(variance + EPS)
    normed = centred * inverse
    return (normed * gain + shift, normed, inverse)

def norm_back(grad_in, normed, inverse, gain):
    scaled = grad_in * gain
    return inverse * (scaled - lax.optimization_barrier(jnp.mean(scaled, axis=-1, keepdims=True)) - normed * lax.optimization_barrier(jnp.mean(scaled * normed, axis=-1, keepdims=True)))

def gelu_exact(values_in):
    return 0.5 * values_in * (1.0 + jax.scipy.special.erf(values_in * 0.7071067811865476))

def gelu_slope(values_in):
    return 0.5 * (1.0 + jax.scipy.special.erf(values_in * 0.7071067811865476)) + values_in * jnp.exp(-0.5 * values_in * values_in) * 0.3989422804014327

def reference(x_in, lengths, w_query, w_key, w_value, w_out, w_up, w_down, b_query, b_value, b_out, b_up, b_down, ln1_gain, ln1_shift, ln2_gain, ln2_shift, d_out):
    f32 = jnp.float32
    bf16 = jnp.bfloat16
    scale = HD ** (-0.5)

    def one_sequence(carry, inputs):
        x_seq, grad_seq, length = inputs
        query = (jnp.dot(x_seq, w_query, preferred_element_type=f32) + b_query).astype(bf16)
        keyed = jnp.dot(x_seq, w_key, preferred_element_type=f32).astype(bf16)
        valued = (jnp.dot(x_seq, w_value, preferred_element_type=f32) + b_value).astype(bf16)
        query_h = query.reshape(L, HEADS, HD).astype(f32)
        key_h = keyed.reshape(L, HEADS, HD).astype(f32)
        value_h = valued.reshape(L, HEADS, HD).astype(f32)
        scores = jnp.einsum('qhd,khd->hqk', query_h, key_h) * scale
        valid = jnp.arange(L, dtype=jnp.int32) < length
        scores = jnp.where(valid[None, None, :], scores, -1e+30)
        top = lax.optimization_barrier(jnp.max(scores, axis=-1, keepdims=True))
        log_total = top + jnp.log(lax.optimization_barrier(jnp.sum(jnp.exp(scores - top), axis=-1, keepdims=True)))
        probs = jnp.exp(scores - log_total)
        probs_b = probs.astype(bf16).astype(f32)
        context = jnp.einsum('hqk,khd->qhd', probs_b, value_h).reshape(L, D).astype(bf16)
        first = x_seq.astype(f32) + jnp.dot(context, w_out, preferred_element_type=f32) + b_out
        hidden, normed_one, inv_one = layer_norm(first, ln1_gain, ln1_shift)
        hidden_b = hidden.astype(bf16)
        upper = jnp.dot(hidden_b, w_up, preferred_element_type=f32) + b_up
        act_b = gelu_exact(upper).astype(bf16)
        second = hidden + jnp.dot(act_b, w_down, preferred_element_type=f32) + b_down
        output, normed_two, inv_two = layer_norm(second, ln2_gain, ln2_shift)
        grad_out = grad_seq.astype(f32)
        dg_two = lax.optimization_barrier(jnp.sum(grad_out * normed_two, axis=0))
        ds_two = lax.optimization_barrier(jnp.sum(grad_out, axis=0))
        d_second = norm_back(grad_out, normed_two, inv_two, ln2_gain)
        db_down = lax.optimization_barrier(jnp.sum(d_second, axis=0))
        d_second_b = d_second.astype(bf16)
        dw_down = jnp.dot(act_b.T, d_second_b, preferred_element_type=f32)
        d_upper = jnp.dot(d_second_b, w_down.T, preferred_element_type=f32) * gelu_slope(upper)
        db_up = lax.optimization_barrier(jnp.sum(d_upper, axis=0))
        d_upper_b = d_upper.astype(bf16)
        dw_up = jnp.dot(hidden_b.T, d_upper_b, preferred_element_type=f32)
        d_hidden = d_second + jnp.dot(d_upper_b, w_up.T, preferred_element_type=f32)
        dg_one = lax.optimization_barrier(jnp.sum(d_hidden * normed_one, axis=0))
        ds_one = lax.optimization_barrier(jnp.sum(d_hidden, axis=0))
        d_first = norm_back(d_hidden, normed_one, inv_one, ln1_gain)
        db_out = lax.optimization_barrier(jnp.sum(d_first, axis=0))
        d_first_b = d_first.astype(bf16)
        dw_out = jnp.dot(context.T, d_first_b, preferred_element_type=f32)
        d_context = jnp.dot(d_first_b, w_out.T, preferred_element_type=f32).astype(bf16)
        d_context_h = d_context.reshape(L, HEADS, HD).astype(f32)
        d_prob = jnp.einsum('qhd,khd->hqk', d_context_h, value_h)
        delta = lax.optimization_barrier(jnp.sum(probs * d_prob, axis=-1, keepdims=True))
        d_score = (probs * (d_prob - delta)).astype(bf16).astype(f32)
        d_query = (jnp.einsum('hqk,khd->qhd', d_score, key_h) * scale).reshape(L, D).astype(bf16)
        d_keys = (jnp.einsum('hqk,qhd->khd', d_score, query_h) * scale).reshape(L, D).astype(bf16)
        d_values = jnp.einsum('hqk,qhd->khd', probs_b, d_context_h).reshape(L, D).astype(bf16)
        dw_query = jnp.dot(x_seq.T, d_query, preferred_element_type=f32)
        dw_key = jnp.dot(x_seq.T, d_keys, preferred_element_type=f32)
        dw_value = jnp.dot(x_seq.T, d_values, preferred_element_type=f32)
        db_query = lax.optimization_barrier(jnp.sum(d_query.astype(f32), axis=0))
        db_value = lax.optimization_barrier(jnp.sum(d_values.astype(f32), axis=0))
        d_in = d_first + jnp.dot(d_query, w_query.T, preferred_element_type=f32) + jnp.dot(d_keys, w_key.T, preferred_element_type=f32) + jnp.dot(d_values, w_value.T, preferred_element_type=f32)
        terms = (dw_query, dw_key, dw_value, dw_out, dw_up, dw_down, db_query, db_value, db_out, db_up, db_down, dg_one, ds_one, dg_two, ds_two)
        new_carry = tuple((total + term for total, term in zip(carry, terms)))
        return (new_carry, (output.astype(bf16), d_in))
    start = (jnp.zeros((D, D), f32), jnp.zeros((D, D), f32), jnp.zeros((D, D), f32), jnp.zeros((D, D), f32), jnp.zeros((D, FF), f32), jnp.zeros((FF, D), f32), jnp.zeros((D,), f32), jnp.zeros((D,), f32), jnp.zeros((D,), f32), jnp.zeros((FF,), f32), jnp.zeros((D,), f32), jnp.zeros((D,), f32), jnp.zeros((D,), f32), jnp.zeros((D,), f32), jnp.zeros((D,), f32))
    totals, stacked = lax.scan(one_sequence, start, (x_in, d_out, lengths))
    block_out, d_input = stacked
    return (block_out, d_input, totals[0], totals[1], totals[2], totals[3], totals[4], totals[5], totals[6], totals[7], totals[8], totals[9], totals[10], totals[11], totals[12], totals[13], totals[14])
```

```python
import jax
import jax.numpy as jnp
from jax import lax
from jax.experimental import pallas as pl
from jax.experimental.pallas import tpu as pltpu
from jax.sharding import PartitionSpec as P

HD = 64
EPS = 1e-05
F32 = jnp.float32
BF = jnp.bfloat16
ANY = pl.BlockSpec(memory_space=pl.ANY)
SMEM = pl.BlockSpec(memory_space=pltpu.SMEM)
VMEM = pl.BlockSpec(memory_space=pltpu.VMEM)


def dot(a, b):
    return jnp.dot(a, b, preferred_element_type=F32)


def dot_nt(a, b):
    return lax.dot_general(a, b, (((1,), (1,)), ((), ())), preferred_element_type=F32)


def dot_tn(a, b):
    return lax.dot_general(a, b, (((0,), (0,)), ((), ())), preferred_element_type=F32)


def sds(shape, dtype):
    return jax.ShapeDtypeStruct(shape, dtype)


def params(mib):
    return pltpu.CompilerParams(vmem_limit_bytes=mib << 20)


def cost(flops, nbytes):
    return pl.CostEstimate(flops=flops, bytes_accessed=nbytes, transcendentals=0)


def xor(value, axis, size, bit):
    return lax.ppermute(value, axis, [(i, i ^ bit) for i in range(size)])


def gather8(own, half):
    swap = lambda v, bit: xor(v, "fsdp", 8, bit)
    by_x, by_y = swap(own, 2), swap(own, 4)
    top, low = swap(by_x[:half], 4), swap(by_y[half:], 2)
    mine = [(own, 0, 0), (by_x, 2, 0), (by_y, 4, 0), (top, 6, 0), (low, 6, half)]
    return mine + [(swap(v, 1), j ^ 1, r) for v, j, r in mine]


def scatter_sum8(keep, send, half):
    add = lambda a, b: a.astype(F32) + b.astype(F32)
    swap = lambda v, bit: xor(v, "fsdp", 8, bit)
    pair = add(keep, swap(send, 1)).astype(BF)
    top_in = swap(pair[1::2, :half], 2)
    low_in = swap(pair[2:, half:], 4)
    top_in2 = swap(add(pair[2, :half], top_in[1]).astype(BF), 4)
    low_in2 = swap(add(pair[1, half:], low_in[1]).astype(BF), 2)
    top = add(pair[0, :half], top_in[0]) + top_in2.astype(F32)
    low = add(pair[0, half:], low_in[0]) + low_in2.astype(F32)
    return jnp.concatenate([top, low], axis=0)


def sum_seq4(value, place):
    rows = value.shape[0]
    value = value.astype(BF)
    kept = []
    for bit, span in ((1, rows // 2), (2, rows // 4)):
        upper = (place // bit) % 2
        mine = lax.dynamic_slice_in_dim(value, upper * span, span)
        other = lax.dynamic_slice_in_dim(value, (1 - upper) * span, span)
        got = xor(other, "seq", 4, bit)
        value = (mine.astype(F32) + got.astype(F32)).astype(BF)
        kept.append(upper)
    for bit, upper in ((2, kept[1]), (1, kept[0])):
        got = xor(value, "seq", 4, bit)
        value = jnp.where(
            upper == 0,
            jnp.concatenate([value, got], axis=0),
            jnp.concatenate([got, value], axis=0),
        )
    return value


class Loader:
    def __init__(self, sems):
        self.sems, self.used = sems, 0

    def start(self, src, dst):
        copy = pltpu.make_async_copy(src, dst, self.sems.at[self.used])
        self.used += 1
        copy.start()
        return copy

    def either(self, cond, src, other, dst):
        first = pltpu.make_async_copy(src, dst, self.sems.at[self.used])
        second = pltpu.make_async_copy(other, dst, self.sems.at[self.used])
        self.used += 1
        pl.when(cond)(first.start)
        pl.when(jnp.logical_not(cond))(second.start)
        return first


def wait_all(copies):
    for copy in copies:
        copy.wait()


def overlap(first, count, low, high):
    start, stop = max(first, low), min(first + count, high)
    return start, max(0, stop - start)


def attend_forward_kernel(info, *refs):
    metas, part, has_bias, lens, seqs = info
    count = len(metas) if metas else 2
    xs = refs[0:4]
    pieces = refs[4 : 4 + count]
    len_ref = refs[4 + count]
    ctx_out = refs[5 + count : 9 + count]
    qkv_out, probs_out, small_out, xf = refs[9 + count : 13 + count]
    w_all, extra, ctx_all, sems = refs[13 + count :]
    f, z = lax.axis_index("fsdp"), lax.axis_index("seq")
    loader = Loader(sems)
    copies = []
    for k in range(4):
        rows = pl.ds(pl.multiple_of((z ^ k) * 128, 128), 128)
        for s in range(2):
            copies.append(loader.start(xs[k].at[s], xf.at[s, rows]))
    if metas:
        tops = {}
        for ref, (j, r0, nrows) in zip(pieces, metas):
            c = f ^ j
            dst = w_all.at[pl.ds(pl.multiple_of(c * part, part), part)]
            if nrows == 4 * part + 16:
                src = ref.at[pl.ds(pl.multiple_of(z * part, part), part)]
                copies.append(loader.start(src, dst))
            elif r0 == 0:
                tops[j] = ref
            else:
                low = pl.multiple_of(jnp.maximum(z - 2, 0) * part, part)
                high = pl.multiple_of(jnp.minimum(z, 1) * part, part)
                copies.append(
                    loader.either(
                        z < 2, tops[j].at[pl.ds(high, part)], ref.at[pl.ds(low, part)], dst
                    )
                )
            if r0 + nrows == 4 * part + 16:
                copies.append(loader.start(ref.at[pl.ds(nrows - 16, 16)], extra.at[c]))
        wait_all(copies)
        blocks = [extra[c].astype(F32) for c in range(8)]
        vectors = jnp.concatenate([b[0:8, 0:part] for b in blocks], axis=1)
        ups = [
            jnp.concatenate([blocks[2 * q][8:9, 0:384], blocks[2 * q + 1][8:9, 0:384]], axis=1)
            for q in range(4)
        ]
        small_out[...] = jnp.concatenate(
            [vectors] + ups + [jnp.zeros((4, 768), F32)], axis=0
        )
    else:
        full, small_in = pieces
        copies.append(loader.start(full.at[z], w_all))
        copies.append(loader.start(small_in, small_out))
        wait_all(copies)
    zero = jnp.zeros((1, 192), F32)
    bias_q, bias_v = zero, zero
    for g in range(4):
        here = (z == g).astype(F32)
        bias_q = bias_q + here * small_out[0:1, g * 192 : (g + 1) * 192]
        bias_v = bias_v + here * small_out[1:2, g * 192 : (g + 1) * 192]
    bias = jnp.concatenate([bias_q, zero, bias_v, jnp.zeros((1, 64), F32)], axis=1)
    for s in range(2):
        qkv = (dot(xf[s], w_all[...]) + bias).astype(BF)
        qkv_out[s] = qkv
        valid = lax.broadcasted_iota(jnp.int32, (1, 512), 1) < len_ref[s]
        heads = []
        for h in range(3):
            q = qkv[:, h * HD : (h + 1) * HD] * jnp.asarray(HD**-0.5, BF)
            k = qkv[:, 192 + h * HD : 192 + (h + 1) * HD]
            v = qkv[:, 384 + h * HD : 384 + (h + 1) * HD]
            scores = jnp.where(valid, dot_nt(q, k), -1e30)
            top = jnp.max(scores, axis=1, keepdims=True)
            e = jnp.exp(scores - top)
            inverse = 1.0 / jnp.sum(e, axis=1, keepdims=True)
            probs = (e * inverse).astype(BF)
            probs_out[s * 3 + h] = probs
            heads.append(dot(probs, v).astype(BF))
        ctx_all[:, s * 192 : (s + 1) * 192] = jnp.concatenate(heads, axis=1)
    for k in range(4):
        ctx_out[k][...] = ctx_all[pl.ds(pl.multiple_of((z ^ k) * 128, 128), 128), :]


def attend_back_kernel(info, *refs):
    split, part = info
    dcs = refs[0:4]
    qkv_in, probs_in, xf = refs[4:7]
    n_out = 2 if split else 2
    dq_out = refs[7:11]
    outs = refs[11 : 11 + n_out]
    dctx, dall, sems = refs[11 + n_out :]
    f, z = lax.axis_index("fsdp"), lax.axis_index("seq")
    loader = Loader(sems)
    copies = []
    for k in range(4):
        rows = pl.ds(pl.multiple_of((z ^ k) * 128, 128), 128)
        copies.append(loader.start(dcs[k], dctx.at[rows]))
    wait_all(copies)
    grad = jnp.zeros((768, 640), F32)
    sums = jnp.zeros((1, 640), F32)
    scale = HD**-0.5
    for s in range(2):
        qs, ks, vs = [], [], []
        for h in range(3):
            q = qkv_in[s, :, h * HD : (h + 1) * HD]
            k = qkv_in[s, :, 192 + h * HD : 192 + (h + 1) * HD]
            v = qkv_in[s, :, 384 + h * HD : 384 + (h + 1) * HD]
            lane = s * 192 + h * HD
            d_ctx = dctx[:, lane : lane + HD]
            probs_b = probs_in[s * 3 + h]
            probs = probs_b.astype(F32)
            d_prob = dot_nt(d_ctx, v)
            delta = jnp.sum(probs * d_prob, axis=1, keepdims=True)
            d_score = (probs * (d_prob - delta)).astype(BF)
            qs.append((dot(d_score, k) * scale).astype(BF))
            ks.append((dot_tn(d_score, q) * scale).astype(BF))
            vs.append(dot_tn(probs_b, d_ctx).astype(BF))
        d_qkv = jnp.concatenate(qs + ks + vs, axis=1)
        dall[:, s * 576 : (s + 1) * 576] = d_qkv
        padded = jnp.concatenate([d_qkv, jnp.zeros((512, 64), BF)], axis=1)
        grad = grad + dot_tn(xf[s], padded)
        sums = sums + jnp.sum(padded.astype(F32), axis=0, keepdims=True)
    for k in range(4):
        dq_out[k][...] = dall[pl.ds(pl.multiple_of((z ^ k) * 128, 128), 128), :]
    grad = grad.astype(BF)
    if split:
        keep, send = outs
        sums = jnp.broadcast_to(sums, (8, 640)).astype(BF)
        for c in range(8):
            slot = (c >> 1) ^ (f >> 1)
            block = jnp.concatenate([grad[c * part : (c + 1) * part], sums], axis=0)

            def put(ref, slot=slot, block=block):
                ref[slot] = block

            pl.when((f & 1) == (c & 1))(lambda put=put: put(keep))
            pl.when((f & 1) != (c & 1))(lambda put=put: put(send))
    else:
        outs[0][...] = grad
        outs[1][...] = jnp.broadcast_to(sums, (8, 640))


def middle_kernel(info, *refs):
    metas, part = info
    count = len(metas) if metas else 3
    x_in, d_out, small, c0, c1, c2, c3 = refs[0:7]
    pieces = refs[7 : 7 + count]
    block_out, d_first_out, d_first_b, act_out, ds_out, hid_out, du_out, sm_out = refs[
        7 + count : 15 + count
    ]
    dctx_out = refs[15 + count : 19 + count]
    w_o, w_u, w_d, slope, sems = refs[19 + count :]
    f, z = lax.axis_index("fsdp"), lax.axis_index("seq")
    loader = Loader(sems)
    out_copies, up_copies, down_copies = [], [], []
    if metas:
        wide = 4 * part
        for ref, (j, r0, nrows) in zip(pieces, metas):
            c = f ^ j
            start, size = overlap(r0, nrows, 0, part)
            if size:
                row = pl.multiple_of(c * part + start, 16)
                out_copies.append(
                    loader.start(ref.at[pl.ds(start - r0, size)], w_o.at[pl.ds(row, size)])
                )
        for ref, (j, r0, nrows) in zip(pieces, metas):
            c = f ^ j
            for q in range(4):
                base = part * (1 + q)
                start, size = overlap(r0, nrows, base, base + part)
                if size:
                    row = pl.multiple_of(c * part + start - base, 16)
                    up_copies.append(
                        loader.start(ref.at[pl.ds(start - r0, size)], w_u.at[q, pl.ds(row, size)])
                    )
        for ref, (j, r0, nrows) in zip(pieces, metas):
            c = f ^ j
            base = part * 5
            start, size = overlap(r0, nrows, base, base + wide)
            if size:
                row = pl.multiple_of(c * wide + start - base, 16)
                down_copies.append(
                    loader.start(ref.at[pl.ds(start - r0, size)], w_d.at[pl.ds(row, size)])
                )
    else:
        out_copies.append(loader.start(pieces[0], w_o))
        up_copies.append(loader.start(pieces[1], w_u))
        down_copies.append(loader.start(pieces[2], w_d))
    row = lambda i: small[i : i + 1, :]
    b_out, b_down, gain1, shift1, gain2, shift2 = (row(i) for i in range(2, 8))
    ctxs = [
        jnp.concatenate([c[:, 0:192], c[:, 192:384]], axis=0)
        for c in (c0[...], c1[...], c2[...], c3[...])
    ]
    group = lambda k: pl.ds(pl.multiple_of((z ^ k) * 192, 64), 192)
    mean = lambda v: jnp.sum(v, axis=1, keepdims=True) * (1.0 / 768.0)
    total = lambda v: jnp.sum(v, axis=0, keepdims=True)

    def norm(value):
        centred = value - mean(value)
        inverse = lax.rsqrt(mean(centred * centred) + EPS)
        return centred * inverse, inverse

    def norm_back(grad, normed, inverse, gain):
        scaled = grad * gain
        return inverse * (scaled - mean(scaled) - normed * mean(scaled * normed))

    wait_all(out_copies)
    first = x_in[...].astype(F32) + b_out
    for k in range(4):
        first = first + dot(ctxs[k], w_o[group(k), :])
    normed1, inverse1 = norm(first)
    hidden = normed1 * gain1 + shift1
    hidden_b = hidden.astype(BF)
    hid_out[...] = hidden_b
    wait_all(up_copies)
    wait_all(down_copies)
    second = hidden + b_down
    for q in range(4):
        cols = slice(q * 768, (q + 1) * 768)
        upper = dot(hidden_b, w_u[q]) + small[8 + q : 9 + q, :]
        half = 0.5 * (1.0 + lax.erf(upper * 0.7071067811865476))
        act = (upper * half).astype(BF)
        act_out[:, cols] = act
        slope[:, cols] = half + upper * jnp.exp(-0.5 * upper * upper) * 0.3989422804014327
        second = second + dot(act, w_d[cols, :])
    normed2, inverse2 = norm(second)
    block_out[...] = (normed2 * gain2 + shift2).astype(BF)
    grad = d_out[...].astype(F32)
    rows = [total(grad * normed2), total(grad)]
    d_second = norm_back(grad, normed2, inverse2, gain2)
    rows.append(total(d_second))
    d_second_b = d_second.astype(BF)
    ds_out[...] = d_second_b
    d_hidden = d_second
    ups = []
    for q in range(4):
        cols = slice(q * 768, (q + 1) * 768)
        d_upper = dot_nt(d_second_b, w_d[cols, :]) * slope[:, cols]
        ups.append(total(d_upper))
        d_upper_b = d_upper.astype(BF)
        du_out[:, cols] = d_upper_b
        d_hidden = d_hidden + dot_nt(d_upper_b, w_u[q])
    rows += [total(d_hidden * normed1), total(d_hidden)]
    d_first = norm_back(d_hidden, normed1, inverse1, gain1)
    rows.append(total(d_first))
    first_b = d_first.astype(BF)
    d_first_out[...] = d_first
    d_first_b[...] = first_b
    for k in range(4):
        d_ctx = dot_nt(first_b, w_o[group(k), :]).astype(BF)
        dctx_out[k][...] = jnp.concatenate([d_ctx[0:128], d_ctx[128:256]], axis=1)
    sm_out[...] = jnp.concatenate(rows + ups + [jnp.zeros((6, 768), F32)], axis=0)


def down_grad_kernel(split, act, d_second_b, *outs):
    f = lax.axis_index("fsdp")
    for c in range(8):
        block = dot_tn(act[:, c * 384 : (c + 1) * 384], d_second_b[...]).astype(BF)
        if split:
            keep, send = outs
            slot = (c >> 1) ^ (f >> 1)

            def put(ref, slot=slot, block=block):
                ref[slot] = block

            pl.when((f & 1) == (c & 1))(lambda put=put: put(keep))
            pl.when((f & 1) != (c & 1))(lambda put=put: put(send))
        else:
            outs[0][c * 384 : (c + 1) * 384] = block


def up_grad_kernel(split, part, hidden_b, du, d_first_b, c0, c1, c2, c3, small, *outs):
    f, z = lax.axis_index("fsdp"), lax.axis_index("seq")

    def route(parity, slot, rows, block):
        keep, send = outs

        def put(ref):
            ref[slot, rows] = block

        pl.when((f & 1) == parity)(lambda: put(keep))
        pl.when((f & 1) != parity)(lambda: put(send))

    for q in range(4):
        grad = dot_tn(hidden_b[...], du[:, q * 768 : (q + 1) * 768]).astype(BF)
        if split:
            for c in range(8):
                slot = (c >> 1) ^ (f >> 1)
                rows = slice(part * q, part * (q + 1))
                route(c & 1, slot, rows, grad[c * part : (c + 1) * part])
        else:
            outs[0][q] = grad
    for k, ref in enumerate((c0, c1, c2, c3)):
        ctx = jnp.concatenate([ref[:, 0:192], ref[:, 192:384]], axis=0)
        grad = dot_tn(ctx, d_first_b[...]).astype(BF)
        if split:
            for i in range(2):
                slot = (z ^ k) ^ (f >> 1)
                rows = slice(part * 4, part * 5)
                route(i, slot, rows, grad[i * part : (i + 1) * part])
        else:
            outs[1][z ^ k] = grad
    if split:
        value = small[...].astype(BF)
        for p in range(4):
            outs[0][p, part * 5 : part * 5 + 16] = value
            outs[1][p, part * 5 : part * 5 + 16] = value


def input_grad_kernel(info, *refs):
    metas, part = info
    count = len(metas) if metas else 1
    d_first, e0, e1, e2, e3 = refs[0:5]
    pieces = refs[5 : 5 + count]
    out = refs[5 + count]
    w_all, sems = refs[6 + count :]
    f, z = lax.axis_index("fsdp"), lax.axis_index("seq")
    loader = Loader(sems)
    copies = []
    if metas:
        for ref, (j, r0, nrows) in zip(pieces, metas):
            c = f ^ j
            for g in range(4):
                start, size = overlap(r0, nrows, g * part, (g + 1) * part)
                if size:
                    row = pl.multiple_of(c * part + start - g * part, 16)
                    copies.append(
                        loader.start(ref.at[pl.ds(start - r0, size)], w_all.at[g, pl.ds(row, size)])
                    )
    else:
        copies.append(loader.start(pieces[0], w_all))
    wait_all(copies)
    total = d_first[...]
    for k, ref in enumerate((e0, e1, e2, e3)):
        d_qkv = jnp.concatenate([ref[:, 0:576], ref[:, 576:1152]], axis=0)
        total = total + dot_nt(d_qkv, w_all[z ^ k][:, 0:576])
    out[...] = total


def build(mesh):
    n, m = mesh.shape["fsdp"], mesh.shape["seq"]
    fast = n == 8
    assert m == 4

    def shards(x_in, lengths, w_query, w_key, w_value, w_out, w_up, w_down, b_query, b_value,
               b_out, b_up, b_down, ln1_gain, ln1_shift, ln2_gain, ln2_shift, d_out):
        f, z = lax.axis_index("fsdp"), lax.axis_index("seq")
        part = w_query.shape[0]
        ff = b_up.shape[0]
        seqs, span, width = x_in.shape
        vectors = (b_query, b_value, b_out, b_down, ln1_gain, ln1_shift, ln2_gain, ln2_shift)
        groups = [
            jnp.concatenate(
                [w[:, g * 192 : (g + 1) * 192] for w in (w_query, w_key, w_value)]
                + [jnp.zeros((part, 64), BF)],
                axis=1,
            )
            for g in range(4)
        ]
        ups = [w_up[:, q * 768 : (q + 1) * 768] for q in range(4)]
        xs = [x_in] + [xor(x_in, "seq", 4, k) for k in (1, 2, 3)]
        if fast:
            vec = jnp.stack(vectors).astype(BF)
            extra = jnp.concatenate(
                [
                    jnp.pad(vec, ((0, 0), (0, 640 - part))),
                    jnp.pad(b_up.astype(BF)[None], ((0, 7), (0, 640 - ff))),
                ],
                axis=0,
            )
            pack1 = jnp.concatenate(groups + [extra], axis=0)
            pieces1 = gather8(pack1, 2 * part)
            pack2 = jnp.concatenate([w_out] + ups + [w_down], axis=0)
            pieces2 = gather8(pack2, 9 * part // 2)
            metas1 = [(j, r, v.shape[0]) for v, j, r in pieces1]
            metas2 = [(j, r, v.shape[0]) for v, j, r in pieces2]
            arrays1 = [v for v, _, _ in pieces1]
            arrays2 = [v for v, _, _ in pieces2]
            first_arrays = arrays1
        else:
            gather = lambda v, axis=0: lax.all_gather(v, "fsdp", axis=axis, tiled=True)
            metas1 = metas2 = None
            full1 = gather(jnp.stack(groups), 1)
            vec = gather(jnp.stack(vectors), 1)
            up_bias = gather(b_up).reshape(4, 768)
            small_in = jnp.concatenate([vec, up_bias, jnp.zeros((4, 768), F32)], axis=0)
            first_arrays = [full1, small_in]
            arrays1 = [full1]
            arrays2 = [gather(w_out), gather(jnp.stack(ups), 1), gather(w_down)]
        n1, n2 = len(first_arrays), len(arrays2)
        outs = pl.pallas_call(
            lambda *r: attend_forward_kernel((metas1, part, True, None, seqs), *r),
            out_shape=[sds((128, 384), BF)] * 4
            + [
                sds((2, 512, 640), BF),
                sds((6, 512, 512), BF),
                sds((16, 768), F32),
                sds((2, 512, 768), BF),
            ],
            in_specs=[ANY] * (4 + n1) + [SMEM],
            out_specs=[VMEM] * 8,
            scratch_shapes=[
                pltpu.VMEM((768, 640), BF),
                pltpu.VMEM((8, 16, 640), BF),
                pltpu.VMEM((512, 384), BF),
                pltpu.SemaphoreType.DMA((40,)),
            ],
            compiler_params=params(40),
            cost_estimate=cost(2000000000, 8000000),
            name="attend_forward",
        )(*xs, *first_arrays, lengths)
        ctx_send, (qkv, probs, small, x_full) = outs[0:4], outs[4:8]
        ctxs = [ctx_send[0]] + [xor(ctx_send[k], "seq", 4, k) for k in (1, 2, 3)]
        tokens = seqs * span
        outs = pl.pallas_call(
            lambda *r: middle_kernel((metas2, part), *r),
            out_shape=[
                sds((tokens, 768), BF),
                sds((tokens, 768), F32),
                sds((tokens, 768), BF),
                sds((tokens, 3072), BF),
                sds((tokens, 768), BF),
                sds((tokens, 768), BF),
                sds((tokens, 3072), BF),
                sds((16, 768), F32),
            ]
            + [sds((128, 384), BF)] * 4,
            in_specs=[VMEM] * 7 + [ANY] * n2,
            out_specs=[VMEM] * 12,
            scratch_shapes=[
                pltpu.VMEM((768, 768), BF),
                pltpu.VMEM((4, 768, 768), BF),
                pltpu.VMEM((3072, 768), BF),
                pltpu.VMEM((tokens, 3072), F32),
                pltpu.SemaphoreType.DMA((80,)),
            ],
            compiler_params=params(48),
            cost_estimate=cost(6000000000, 20000000),
            name="middle",
        )(x_in.reshape(tokens, width), d_out.reshape(tokens, width), small, *ctxs, *arrays2)
        block_out, d_first, d_first_b, act, d_second_b, hidden_b, du, small_grad = outs[0:8]
        dctx_send = outs[8:12]
        dctxs = [dctx_send[0]] + [xor(dctx_send[k], "seq", 4, k) for k in (1, 2, 3)]
        down = pl.pallas_call(
            lambda *r: down_grad_kernel(fast, *r),
            out_shape=[sds((4, 384, 768), BF)] * 2 if fast else [sds((3072, 768), BF)],
            compiler_params=params(32),
            cost_estimate=cost(1200000000, 7000000),
            name="down_grad",
        )(act, d_second_b)
        rows2 = part * 5 + 16
        up = pl.pallas_call(
            lambda *r: up_grad_kernel(fast, part, *r),
            out_shape=[sds((4, rows2, 768), BF)] * 2
            if fast
            else [sds((4, 768, 768), BF), sds((4, 192, 768), BF)],
            compiler_params=params(32),
            cost_estimate=cost(1500000000, 9000000),
            name="up_grad",
        )(hidden_b, du, d_first_b, *ctxs, small_grad)
        outs = pl.pallas_call(
            lambda *r: attend_back_kernel((fast, part), *r),
            out_shape=[sds((128, 1152), BF)] * 4
            + (
                [sds((4, part + 8, 640), BF)] * 2
                if fast
                else [sds((768, 640), BF), sds((8, 640), F32)]
            ),
            in_specs=[ANY] * 4 + [VMEM] * 3,
            out_specs=[VMEM] * 6,
            scratch_shapes=[
                pltpu.VMEM((512, 384), BF),
                pltpu.VMEM((512, 1152), BF),
                pltpu.SemaphoreType.DMA((4,)),
            ],
            compiler_params=params(40),
            cost_estimate=cost(4000000000, 10000000),
            name="attend_back",
        )(*dctxs, qkv, probs, x_full)
        dq_send, (qkv_a, qkv_b) = outs[0:4], outs[4:6]
        dqs = [dq_send[0]] + [xor(dq_send[k], "seq", 4, k) for k in (1, 2, 3)]
        d_input = pl.pallas_call(
            lambda *r: input_grad_kernel((metas1, part), *r),
            out_shape=sds((tokens, 768), F32),
            in_specs=[VMEM] * 5 + [ANY] * len(arrays1),
            out_specs=VMEM,
            scratch_shapes=[pltpu.VMEM((4, 768, 640), BF), pltpu.SemaphoreType.DMA((40,))],
            compiler_params=params(24),
            cost_estimate=cost(1000000000, 8000000),
            name="input_grad",
        )(d_first, *dqs, *arrays1)
        if fast:
            dw_down = sum_seq4(scatter_sum8(down[0], down[1], 192), z).astype(F32)
            second = sum_seq4(scatter_sum8(up[0], up[1], rows2 // 2), z).astype(F32)
            mine = scatter_sum8(qkv_a, qkv_b, 48).astype(BF)
            rel = jnp.stack([mine] + [xor(mine, "seq", 4, k) for k in (1, 2, 3)])
            dw_up = jnp.concatenate([second[q * part : (q + 1) * part] for q in range(4)], axis=1)
            dw_out = second[4 * part : 5 * part]
            sums = second[5 * part : 5 * part + 16]
            by_group = jnp.stack([lax.dynamic_index_in_dim(rel, z ^ g, 0, False) for g in range(4)])
            by_group = by_group.astype(F32)
            dw_qkv = by_group[:, 0:part]
            qkv_sums = by_group[:, part]
            column = lambda v: lax.dynamic_slice_in_dim(v, f * part, part)
        else:
            both = ("fsdp", "seq")
            reduce = lambda v, axis=0: lax.psum(
                lax.psum_scatter(v.astype(BF), "fsdp", scatter_dimension=axis, tiled=True), "seq"
            ).astype(F32)
            dw_down = reduce(down[0])
            up4 = reduce(up[0], 1)
            dw_up = jnp.concatenate([up4[q] for q in range(4)], axis=1)
            dw_out = reduce(up[1].reshape(768, 768))
            sums = lax.psum(small_grad, both)
            mine = lax.psum_scatter(qkv_a, "fsdp", scatter_dimension=0, tiled=True)
            dw_qkv = lax.all_gather(mine, "seq").astype(F32)
            qkv_sums = lax.all_gather(lax.psum(qkv_b[0], "fsdp"), "seq")
            column = lambda v: lax.dynamic_slice_in_dim(v, f * part, part)
        weight = lambda i: jnp.concatenate(
            [dw_qkv[g, :, i * 192 : (i + 1) * 192] for g in range(4)], axis=1
        )
        bias = lambda i: column(qkv_sums[:, i * 192 : (i + 1) * 192].reshape(768))
        db_up = lax.dynamic_slice_in_dim(sums[6:10].reshape(3072), f * ff, ff)
        return (
            block_out.reshape(seqs, span, width),
            d_input.reshape(seqs, span, width),
            weight(0),
            weight(1),
            weight(2),
            dw_out,
            dw_up,
            dw_down,
            bias(0),
            bias(2),
            column(sums[5]),
            db_up,
            column(sums[2]),
            column(sums[3]),
            column(sums[4]),
            column(sums[0]),
            column(sums[1]),
        )

    return shards


def solution(mesh):
    rows, cols, flat = P("fsdp", "seq", None), P("fsdp", None), P("fsdp")
    return jax.shard_map(
        build(mesh),
        mesh=mesh,
        in_specs=(rows, flat) + (cols,) * 6 + (flat,) * 9 + (rows,),
        out_specs=(rows, rows) + (cols,) * 6 + (flat,) * 9,
        check_vma=False,
    )
```
